256 devices in a mesh: seq: 32 (over x, y, core), head: 8 (over z).
Axes of the slice: x: 4, y: 4, z: 8, core: 2. Of those that a mesh axis runs over, the one named last changes fastest.
Arguments:
- queries: bfloat16 [32768, 32, 128], P(('seq', 'head')), may hold values from -48 to 48
- keys_in: bfloat16 [32768, 32, 128], P(('seq', 'head')), may hold values from -48 to 48
- values: bfloat16 [32768, 32, 128], P(('seq', 'head')), may hold values from -48 to 48
- cotangent: bfloat16 [32768, 32, 128], P(('seq', 'head')), may hold values from -48 to 48
Outputs:
- attended: bfloat16 [32768, 32, 128], P('seq', 'head')
- grad_queries: bfloat16 [32768, 32, 128], P('seq', 'head')
- grad_keys: bfloat16 [32768, 32, 128], P('seq', 'head')
- grad_values: bfloat16 [32768, 32, 128], P('seq', 'head')
The draws below stay inside these ranges and needn't reach their ends.
All inputs are finite; a program needn't handle non-finite values.
Results may differ from the reference program's by a relative error of at most 0.01.
Values may be sent and summed in bfloat16 or wider, within the bound.
A program may use at most 128 MiB of HBM per device.

```python
import jax
import jax.numpy as jnp
from jax import lax

HEADS = 32
DH = 128
BLOCK = 512
OFFSET = 1048576
SEQ = 32768


def steps_of(rng, shape, cuts, least, top_value):
    def one(dim, blocks):
        steps = jax.random.uniform(jax.random.fold_in(jax.random.fold_in(rng, 6), dim), (blocks,), jnp.float32, least / len(cuts), top_value / len(cuts))
        return jnp.repeat(jnp.exp(steps), shape[dim] // blocks).reshape((-1,) + (1,) * (len(shape) - dim - 1))

    loudness = one(*cuts[0])
    for cut in cuts[1:]:
        loudness = loudness * one(*cut)
    return loudness


def bell_draw(rng, shape, deviation, bound, cuts=(), kind=jnp.bfloat16):
    gain = steps_of(rng, shape, cuts, -0.22, 0.18) if cuts else 1.0
    values = jax.random.normal(rng, shape, jnp.float32) * deviation * gain
    return jnp.minimum(jnp.maximum(values, -bound), bound).astype(kind)


def setup_inputs(seed: int = 0) -> dict:
    key_of = jax.random.split(jax.random.key(seed), 5)
    queries = bell_draw(key_of[0], (SEQ, HEADS, DH), 8.0, 48.0, ((0, 256),))
    keys_in = bell_draw(key_of[1], (SEQ, HEADS, DH), 8.0, 48.0, ((0, 256),))
    values = bell_draw(key_of[2], (SEQ, HEADS, DH), 8.0, 48.0, ((0, 256),))
    cotangent = bell_draw(key_of[3], (SEQ, HEADS, DH), 8.0, 48.0, ((0, 256),))
    return {"queries": queries, "keys_in": keys_in, "values": values, "cotangent": cotangent}


def reference(queries, keys_in, values, cotangent):
    block_count = SEQ // BLOCK
    position = (jnp.arange(SEQ, dtype=jnp.int32) + OFFSET + 1).astype(jnp.float32)
    scaled_grad = (cotangent.astype(jnp.float32) / position[:, None, None]).astype(jnp.bfloat16)
    causal_mask = jnp.arange(BLOCK)[:, None] >= jnp.arange(BLOCK)[None, :]

    def to_blocks(array):
        return array.reshape(block_count, BLOCK, HEADS, DH)

    sequence_blocks = (to_blocks(queries), to_blocks(keys_in), to_blocks(values), to_blocks(scaled_grad), position.reshape(block_count, BLOCK))

    def masked_scores(left_side, right_side):
        raw_scores = jnp.einsum('thd,shd->hts', left_side, right_side)
        return jnp.where(causal_mask[None], raw_scores, 0.0).astype(jnp.bfloat16).astype(jnp.float32)

    def widen(block_data):
        return [part.astype(jnp.float32) for part in block_data[:4]]

    def forward(carried, block_data):
        query_wide, key_wide, value_wide, grad_wide = widen(block_data)
        state_used = carried.astype(jnp.bfloat16).astype(jnp.float32)
        attention = masked_scores(query_wide, key_wide)
        grad_scores = masked_scores(grad_wide, value_wide)
        result = jnp.einsum('thd,hde->the', query_wide, state_used) + jnp.einsum('hts,she->the', attention, value_wide)
        result = result / block_data[4][:, None, None]
        grad_query = jnp.einsum('the,hde->thd', grad_wide, state_used) + jnp.einsum('hts,shd->thd', grad_scores, key_wide)
        carried = carried + jnp.einsum('shd,she->hde', key_wide, value_wide)
        return carried, (result.astype(jnp.bfloat16), grad_query.astype(jnp.bfloat16))

    def backward(carried, block_data):
        query_wide, key_wide, value_wide, grad_wide = widen(block_data)
        state_used = carried.astype(jnp.bfloat16).astype(jnp.float32)
        attention = masked_scores(query_wide, key_wide)
        grad_scores = masked_scores(grad_wide, value_wide)
        grad_key = jnp.einsum('she,hde->shd', value_wide, state_used) + jnp.einsum('hts,thd->shd', grad_scores, query_wide)
        grad_value = jnp.einsum('shd,hde->she', key_wide, state_used) + jnp.einsum('hts,the->she', attention, grad_wide)
        carried = carried + jnp.einsum('thd,the->hde', query_wide, grad_wide)
        return carried, (grad_key.astype(jnp.bfloat16), grad_value.astype(jnp.bfloat16))

    zero_state = jnp.zeros((HEADS, DH, DH), jnp.float32)
    final_state, (attended, grad_queries) = lax.scan(forward, zero_state, sequence_blocks)
    final_other, (grad_keys, grad_values) = lax.scan(backward, zero_state, sequence_blocks, reverse=True)
    shape_out = (SEQ, HEADS, DH)
    return (attended.reshape(shape_out), grad_queries.reshape(shape_out), grad_keys.reshape(shape_out), grad_values.reshape(shape_out))
```

```python
import functools

import jax
import jax.numpy as jnp
from jax import lax
from jax.experimental import pallas as pl
from jax.experimental.pallas import tpu as pltpu
from jax.sharding import PartitionSpec as P

BLOCK = 512
OFFSET = 1048576
MESH = pl.DeviceIdType.MESH
NZ = 8
NX = 4
NY = 4
ROWS = 128
HALF = 64
FAR_FIRST = (4, 3, 5, 2, 6, 1, 7)
F32 = jnp.float32
BF16 = jnp.bfloat16


def dot(a, b, dims):
    return lax.dot_general(a, b, (dims, ((), ())), preferred_element_type=F32)


NN = ((1,), (0,))
NT = ((1,), (1,))
TN = ((0,), (0,))


def exchange_kernel(
    q_ref, k_ref, v_ref, g_ref, rows_out, states_out,
    inb, stg, sbuf, rbuf, recip, own, csend, cbuf, ysend, ybuf, xsend, xbuf, fsend, fbuf, stout,
    in_sem, s0_sem, r0_sem, s_sem, r_sem, l_sem, o_sem, st_sem,
    cs_sem, cr_sem, ys_sem, yr_sem, xs_sem, xr_sem, fs_sem, fr_sem,
):
    z = lax.axis_index("head")
    seq = lax.axis_index("seq")
    core = lax.rem(seq, 2)
    chip = seq // 2
    y = lax.rem(chip, NY)
    x = chip // NY
    partner = seq + 1 - 2 * core

    def y_peer(d):
        return (x * NY + lax.rem(y + d, NY)) * 2 + core

    def x_peer(d):
        return (lax.rem(x + d, NX) * NY + y) * 2 + core

    loads = []
    for a, ref in enumerate((k_ref, v_ref, q_ref, g_ref)):
        copy = pltpu.make_async_copy(ref, inb.at[a], in_sem.at[a])
        copy.start()
        loads.append(copy)

    barrier = pltpu.get_barrier_semaphore()
    for d in range(1, NZ):
        pl.semaphore_signal(
            barrier, inc=1, device_id={"head": lax.rem(z + d, NZ)}, device_id_type=MESH
        )
    for peer in [y_peer(d) for d in (1, 2, 3)] + [x_peer(d) for d in (1, 2, 3)] + [partner]:
        pl.semaphore_signal(barrier, inc=1, device_id={"seq": peer}, device_id_type=MESH)

    first_row = (seq * NZ + z) * ROWS + OFFSET + 1
    position = (first_row + lax.broadcasted_iota(jnp.int32, (ROWS, 128), 0)).astype(F32)
    recip[...] = 1.0 / position

    def head_major(hl, a):
        for dest in range(NZ):
            part = stg[a, pl.ds(dest * 4 + hl, ROWS, stride=32), :]
            if a == 3:
                part = part * recip[...]
            sbuf[hl, dest, a] = part.astype(BF16)

    def first_copy(a, d):
        dest = lax.rem(z + d, NZ)
        return pltpu.make_async_remote_copy(
            src_ref=sbuf.at[0, dest, a],
            dst_ref=rbuf.at[0, a, pl.ds(pl.multiple_of(z * ROWS, ROWS), ROWS), :],
            send_sem=s0_sem.at[a, d],
            recv_sem=r0_sem.at[a, d],
            device_id={"head": dest},
            device_id_type=MESH,
        )

    def stage_copy(hl, d):
        dest = lax.rem(z + d, NZ)
        return pltpu.make_async_remote_copy(
            src_ref=sbuf.at[hl, dest],
            dst_ref=rbuf.at[hl, :, pl.ds(pl.multiple_of(z * ROWS, ROWS), ROWS), :],
            send_sem=s_sem.at[hl, d],
            recv_sem=r_sem.at[hl, d],
            device_id={"head": dest},
            device_id_type=MESH,
        )

    def local_copy(hl):
        return pltpu.make_async_copy(
            sbuf.at[hl, z],
            rbuf.at[hl, :, pl.ds(pl.multiple_of(z * ROWS, ROWS), ROWS), :],
            l_sem.at[hl],
        )

    for a in range(4):
        loads[a].wait()
        stg[a] = inb[a].astype(F32)
        head_major(0, a)
        if a == 0:
            pl.semaphore_wait(barrier, 14)
        for d in FAR_FIRST:
            first_copy(a, d).start()
    local_copy(0).start()
    for hl in range(1, 4):
        for a in range(4):
            head_major(hl, a)
        for d in FAR_FIRST:
            stage_copy(hl, d).start()
        local_copy(hl).start()

    def c_copy(hl):
        return pltpu.make_async_remote_copy(
            src_ref=csend.at[hl], dst_ref=cbuf.at[hl],
            send_sem=cs_sem.at[hl], recv_sem=cr_sem.at[hl],
            device_id={"seq": partner}, device_id_type=MESH,
        )

    def y_copy(hl, d):
        return pltpu.make_async_remote_copy(
            src_ref=ysend.at[hl], dst_ref=ybuf.at[hl, y],
            send_sem=ys_sem.at[hl, d], recv_sem=yr_sem.at[hl, d],
            device_id={"seq": y_peer(d)}, device_id_type=MESH,
        )

    def x_copy(hl, d):
        later = (lax.rem(x + d, NX) > x).astype(jnp.int32)
        return pltpu.make_async_remote_copy(
            src_ref=xsend.at[hl, 1 - later], dst_ref=xbuf.at[hl, x],
            send_sem=xs_sem.at[hl, d], recv_sem=xr_sem.at[hl, d],
            device_id={"seq": x_peer(d)}, device_id_type=MESH,
        )

    def f_copy(hl):
        return pltpu.make_async_remote_copy(
            src_ref=fsend.at[hl], dst_ref=fbuf.at[hl],
            send_sem=fs_sem.at[hl], recv_sem=fr_sem.at[hl],
            device_id={"seq": partner}, device_id_type=MESH,
        )

    mine = pl.ds(pl.multiple_of(core * HALF, HALF), HALF)
    other = pl.ds(pl.multiple_of((1 - core) * HALF, HALF), HALF)
    outs = []
    for hl in range(4):
        if hl == 0:
            for a in range(4):
                for d in FAR_FIRST:
                    first_copy(a, d).wait_recv()
        else:
            for d in FAR_FIRST:
                stage_copy(hl, d).wait_recv()
        local_copy(hl).wait()
        out = pltpu.make_async_copy(rbuf.at[hl], rows_out.at[hl], o_sem.at[hl])
        out.start()
        outs.append(out)
        for b in range(2):
            rows = pl.ds(b * BLOCK, BLOCK)
            own[b] = dot(rbuf[hl, 0, rows, :], rbuf[hl, 1, rows, :], TN)
            own[2 + b] = dot(rbuf[hl, 2, rows, :], rbuf[hl, 3, rows, :], TN)
        csend[hl, 0] = (own[0, other, :] + own[1, other, :]).astype(BF16)
        csend[hl, 1] = (own[2, other, :] + own[3, other, :]).astype(BF16)
        c_copy(hl).start()
        own_kv = own[0, mine, :] + own[1, mine, :]
        own_qg = own[2, mine, :] + own[3, mine, :]
        c_copy(hl).wait_recv()
        pair_kv = cbuf[hl, 0].astype(F32)
        pair_qg = cbuf[hl, 1].astype(F32)
        chip_kv = own_kv + pair_kv
        chip_qg = own_qg + pair_qg
        ysend[hl, 0] = chip_kv.astype(BF16)
        ysend[hl, 1] = chip_qg.astype(BF16)
        for d in (2, 1, 3):
            y_copy(hl, d).start()
        for d in (1, 3, 2):
            y_copy(hl, d).wait_recv()
        row_kv = chip_kv
        row_qg = chip_qg
        before = jnp.zeros((HALF, 128), F32)
        after = jnp.zeros((HALF, 128), F32)
        for d in (1, 2, 3):
            source = lax.rem(y + d, NY)
            got_kv = ybuf[hl, source, 0].astype(F32)
            got_qg = ybuf[hl, source, 1].astype(F32)
            row_kv = row_kv + got_kv
            row_qg = row_qg + got_qg
            before = before + jnp.where(source < y, got_kv, 0.0)
            after = after + jnp.where(source > y, got_qg, 0.0)
        xsend[hl, 0] = row_kv.astype(BF16)
        xsend[hl, 1] = row_qg.astype(BF16)
        for d in (2, 1, 3):
            x_copy(hl, d).start()
        for d in (1, 3, 2):
            x_copy(hl, d).wait_recv()
        for d in (1, 2, 3):
            source = lax.rem(x + d, NX)
            got = xbuf[hl, source].astype(F32)
            before = before + jnp.where(source < x, got, 0.0)
            after = after + jnp.where(source > x, got, 0.0)
        fsend[hl, 0] = (before + jnp.where(core == 0, own_kv, 0.0)).astype(BF16)
        fsend[hl, 1] = (after + jnp.where(core == 1, own_qg, 0.0)).astype(BF16)
        f_copy(hl).start()
        before = before + jnp.where(core == 1, pair_kv, 0.0)
        after = after + jnp.where(core == 0, pair_qg, 0.0)
        stout[hl, 0, mine, :] = before.astype(BF16)
        stout[hl, 1, mine, :] = (before + own[0, mine, :]).astype(BF16)
        stout[hl, 2, mine, :] = (after + own[3, mine, :]).astype(BF16)
        stout[hl, 3, mine, :] = after.astype(BF16)
        f_copy(hl).wait_recv()
        before = fbuf[hl, 0].astype(F32)
        after = fbuf[hl, 1].astype(F32)
        stout[hl, 0, other, :] = before.astype(BF16)
        stout[hl, 1, other, :] = (before + own[0, other, :]).astype(BF16)
        stout[hl, 2, other, :] = (after + own[3, other, :]).astype(BF16)
        stout[hl, 3, other, :] = after.astype(BF16)
        out = pltpu.make_async_copy(stout.at[hl], states_out.at[hl], st_sem.at[hl])
        out.start()
        outs.append(out)
    for hl in range(4):
        for d in FAR_FIRST:
            if hl == 0:
                for a in range(4):
                    first_copy(a, d).wait_send()
            else:
                stage_copy(hl, d).wait_send()
        c_copy(hl).wait_send()
        f_copy(hl).wait_send()
        for d in (1, 2, 3):
            y_copy(hl, d).wait_send()
            x_copy(hl, d).wait_send()
    for out in outs:
        out.wait()


def exchange(queries, keys_in, values, cotangent):
    flat = [a.reshape(ROWS * 32, 128) for a in (queries, keys_in, values, cotangent)]
    any_space = pl.BlockSpec(memory_space=pl.ANY)
    dma = pltpu.SemaphoreType.DMA
    return pl.pallas_call(
        exchange_kernel,
        out_shape=(
            jax.ShapeDtypeStruct((4, 4, 1024, 128), BF16),
            jax.ShapeDtypeStruct((4, 4, 128, 128), BF16),
        ),
        in_specs=[any_space] * 4,
        out_specs=(any_space, any_space),
        scratch_shapes=[
            pltpu.VMEM((4, ROWS * 32, 128), BF16),
            pltpu.VMEM((4, ROWS * 32, 128), F32),
            pltpu.VMEM((4, NZ, 4, ROWS, 128), BF16),
            pltpu.VMEM((4, 4, 1024, 128), BF16),
            pltpu.VMEM((ROWS, 128), F32),
            pltpu.VMEM((4, 128, 128), F32),
            pltpu.VMEM((4, 2, HALF, 128), BF16),
            pltpu.VMEM((4, 2, HALF, 128), BF16),
            pltpu.VMEM((4, 2, HALF, 128), BF16),
            pltpu.VMEM((4, NY, 2, HALF, 128), BF16),
            pltpu.VMEM((4, 2, HALF, 128), BF16),
            pltpu.VMEM((4, NX, HALF, 128), BF16),
            pltpu.VMEM((4, 2, HALF, 128), BF16),
            pltpu.VMEM((4, 2, HALF, 128), BF16),
            pltpu.VMEM((4, 4, 128, 128), BF16),
            dma((4,)), dma((4, NZ)), dma((4, NZ)), dma((4, NZ)), dma((4, NZ)),
            dma((4,)), dma((4,)), dma((4,)),
            dma((4,)), dma((4,)), dma((4, 4)), dma((4, 4)), dma((4, 4)), dma((4, 4)),
            dma((4,)), dma((4,)),
        ],
        compiler_params=pltpu.CompilerParams(
            collective_id=0, has_side_effects=True, vmem_limit_bytes=63 << 20
        ),
        name="exchange",
    )(*flat)


def blocks_kernel(rows_ref, states_ref, att_ref, gq_ref, gk_ref, gv_ref, acc):
    b = pl.program_id(0)
    h = pl.program_id(1)
    seq = lax.axis_index("seq")
    k, v, q, g = (rows_ref[0, a] for a in range(4))
    before = states_ref[0, b]
    after = states_ref[0, 2 + b]
    mask = lax.broadcasted_iota(jnp.int32, (BLOCK, BLOCK), 0) >= lax.broadcasted_iota(
        jnp.int32, (BLOCK, BLOCK), 1
    )
    score = jnp.where(mask, dot(q, k, NT), 0.0).astype(BF16)
    grad_score = jnp.where(mask, dot(g, v, NT), 0.0).astype(BF16)
    position = (
        seq * 1024 + b * BLOCK + OFFSET + 1
        + lax.broadcasted_iota(jnp.int32, (BLOCK, 128), 0)
    ).astype(F32)
    mine = pl.ds(h, BLOCK, stride=4)
    acc[0, mine, :] = (dot(q, before, NN) + dot(score, v, NN)) / position
    acc[1, mine, :] = dot(g, before, NT) + dot(grad_score, k, NN)
    acc[2, mine, :] = dot(v, after, NT) + dot(grad_score, q, TN)
    acc[3, mine, :] = dot(k, after, NN) + dot(score, g, TN)

    @pl.when(h == 3)
    def _():
        att_ref[...] = acc[0].astype(BF16)
        gq_ref[...] = acc[1].astype(BF16)
        gk_ref[...] = acc[2].astype(BF16)
        gv_ref[...] = acc[3].astype(BF16)


def block_outputs(rows, states):
    out = jax.ShapeDtypeStruct((4096, 128), BF16)
    out_spec = pl.BlockSpec((BLOCK * 4, 128), lambda b, h: (b, 0))
    results = pl.pallas_call(
        blocks_kernel,
        out_shape=(out,) * 4,
        grid=(2, 4),
        in_specs=[
            pl.BlockSpec((1, 4, BLOCK, 128), lambda b, h: (h, 0, b, 0)),
            pl.BlockSpec((1, 4, 128, 128), lambda b, h: (h, 0, 0, 0)),
        ],
        out_specs=(out_spec,) * 4,
        scratch_shapes=[pltpu.VMEM((4, BLOCK * 4, 128), F32)],
        compiler_params=pltpu.CompilerParams(vmem_limit_bytes=40 << 20),
        name="blocks",
    )(rows, states)
    return tuple(r.reshape(1024, 4, 128) for r in results)


def shards(queries, keys_in, values, cotangent):
    rows, states = exchange(queries, keys_in, values, cotangent)
    return block_outputs(rows, states)


def solution(mesh):
    in_specs = (P(("seq", "head"), None, None),) * 4
    out_specs = (P("seq", "head", None),) * 4
    return jax.shard_map(shards, mesh=mesh, in_specs=in_specs, out_specs=out_specs, check_vma=False)
```

```python
import functools

import jax
import jax.numpy as jnp
from jax import lax
from jax.experimental import pallas as pl
from jax.experimental.pallas import tpu as pltpu
from jax.sharding import PartitionSpec as P

BLOCK = 512
OFFSET = 1048576
MESH = pl.DeviceIdType.MESH
NZ = 8
NX = 4
NY = 4
ROWS = 128
HALF = 64
STRIP = 256
FAR_FIRST = (4, 3, 5, 2, 6, 1, 7)
F32 = jnp.float32
BF16 = jnp.bfloat16


def dot(a, b, dims):
    return lax.dot_general(a, b, (dims, ((), ())), preferred_element_type=F32)


NN = ((1,), (0,))
NT = ((1,), (1,))
TN = ((0,), (0,))


def exchange_kernel(
    q_ref, k_ref, v_ref, g_ref, out_ref,
    inb, stg, sbuf, rbuf, recip, recip_out, own, part, before_used, after_used,
    csend, cbuf, ysend, ybuf, xsend, xbuf, fsend, fbuf,
    in_sem, s_sem, r_sem, l_sem,
    cs_sem, cr_sem, ys_sem, yr_sem, xs_sem, xr_sem, fs_sem, fr_sem,
):
    z = lax.axis_index("head")
    seq = lax.axis_index("seq")
    core = lax.rem(seq, 2)
    chip = seq // 2
    y = lax.rem(chip, NY)
    x = chip // NY
    partner = seq + 1 - 2 * core

    def y_peer(d):
        return (x * NY + lax.rem(y + d, NY)) * 2 + core

    def x_peer(d):
        return (lax.rem(x + d, NX) * NY + y) * 2 + core

    loads = []
    for a, ref in enumerate((k_ref, v_ref, q_ref, g_ref)):
        copy = pltpu.make_async_copy(ref, inb.at[a], in_sem.at[a])
        copy.start()
        loads.append(copy)

    barrier = pltpu.get_barrier_semaphore()
    for d in range(1, NZ):
        pl.semaphore_signal(
            barrier, inc=1, device_id={"head": lax.rem(z + d, NZ)}, device_id_type=MESH
        )
    for peer in [y_peer(d) for d in (1, 2, 3)] + [x_peer(d) for d in (1, 2, 3)] + [partner]:
        pl.semaphore_signal(barrier, inc=1, device_id={"seq": peer}, device_id_type=MESH)

    first_row = (seq * NZ + z) * ROWS + OFFSET + 1
    position = (first_row + lax.broadcasted_iota(jnp.int32, (ROWS, 128), 0)).astype(F32)
    recip[...] = 1.0 / position

    def head_major(hl, a):
        for dest in range(NZ):
            piece = stg[a, pl.ds(dest * 4 + hl, ROWS, stride=32), :]
            if a == 3:
                piece = piece * recip[...]
            sbuf[hl, dest, a] = piece.astype(BF16)

    here = pl.ds(pl.multiple_of(z * ROWS, ROWS), ROWS)

    def z_copy(hl, a, d):
        dest = lax.rem(z + d, NZ)
        return pltpu.make_async_remote_copy(
            src_ref=sbuf.at[hl, dest, a],
            dst_ref=rbuf.at[hl, a, here, :],
            send_sem=s_sem.at[hl, a, d],
            recv_sem=r_sem.at[hl, a, d],
            device_id={"head": dest},
            device_id_type=MESH,
        )

    def local_copy(hl):
        return pltpu.make_async_copy(sbuf.at[hl, z], rbuf.at[hl, :, here, :], l_sem.at[hl])

    for a in range(4):
        loads[a].wait()
        stg[a] = inb[a].astype(F32)
        head_major(0, a)
        if a == 0:
            pl.semaphore_wait(barrier, 14)
        for d in FAR_FIRST:
            z_copy(0, a, d).start()
    local_copy(0).start()
    for hl in range(1, 4):
        for a in range(4):
            head_major(hl, a)
            for d in FAR_FIRST:
                z_copy(hl, a, d).start()
        local_copy(hl).start()

    position = (
        seq * 1024 + OFFSET + 1 + lax.broadcasted_iota(jnp.int32, (1024, 128), 0)
    ).astype(F32)
    recip_out[...] = 1.0 / position

    def c_copy(hl):
        return pltpu.make_async_remote_copy(
            src_ref=csend.at[hl], dst_ref=cbuf.at[hl],
            send_sem=cs_sem.at[hl], recv_sem=cr_sem.at[hl],
            device_id={"seq": partner}, device_id_type=MESH,
        )

    def y_copy(hl, d):
        return pltpu.make_async_remote_copy(
            src_ref=ysend.at[hl], dst_ref=ybuf.at[hl, y],
            send_sem=ys_sem.at[hl, d], recv_sem=yr_sem.at[hl, d],
            device_id={"seq": y_peer(d)}, device_id_type=MESH,
        )

    def x_copy(hl, d):
        later = (lax.rem(x + d, NX) > x).astype(jnp.int32)
        return pltpu.make_async_remote_copy(
            src_ref=xsend.at[hl, 1 - later], dst_ref=xbuf.at[hl, x],
            send_sem=xs_sem.at[hl, d], recv_sem=xr_sem.at[hl, d],
            device_id={"seq": x_peer(d)}, device_id_type=MESH,
        )

    def f_copy(hl):
        return pltpu.make_async_remote_copy(
            src_ref=fsend.at[hl], dst_ref=fbuf.at[hl],
            send_sem=fs_sem.at[hl], recv_sem=fr_sem.at[hl],
            device_id={"seq": partner}, device_id_type=MESH,
        )

    mine = pl.ds(pl.multiple_of(core * HALF, HALF), HALF)
    other = pl.ds(pl.multiple_of((1 - core) * HALF, HALF), HALF)

    def within_block(hl, b):
        for t in range(2):
            rows = pl.ds(b * BLOCK + t * STRIP, STRIP)
            reach = (t + 1) * STRIP
            seen = pl.ds(b * BLOCK, reach)
            k, v = rbuf[hl, 0, seen, :], rbuf[hl, 1, seen, :]
            q, g = rbuf[hl, 2, rows, :], rbuf[hl, 3, rows, :]
            mask = t * STRIP + lax.broadcasted_iota(
                jnp.int32, (STRIP, reach), 0
            ) >= lax.broadcasted_iota(jnp.int32, (STRIP, reach), 1)
            score = jnp.where(mask, dot(q, k, NT), 0.0).astype(BF16)
            grad_score = jnp.where(mask, dot(g, v, NT), 0.0).astype(BF16)
            part[0, rows, :] = dot(score, v, NN)
            part[1, rows, :] = dot(grad_score, k, NN)
            grad_key = dot(grad_score, q, TN)
            grad_value = dot(score, g, TN)
            if t:
                first = pl.ds(b * BLOCK, STRIP)
                part[2, first, :] += grad_key[:STRIP]
                part[3, first, :] += grad_value[:STRIP]
            part[2, rows, :] = grad_key[t * STRIP :]
            part[3, rows, :] = grad_value[t * STRIP :]

    def head(hl, carry):
        for a in (0, 1):
            for d in FAR_FIRST:
                z_copy(hl, a, d).wait_recv()
        local_copy(hl).wait()
        for b in range(2):
            rows = pl.ds(b * BLOCK, BLOCK)
            own[b] = dot(rbuf[hl, 0, rows, :], rbuf[hl, 1, rows, :], TN)
        for a in (2, 3):
            for d in FAR_FIRST:
                z_copy(hl, a, d).wait_recv()
        for b in range(2):
            rows = pl.ds(b * BLOCK, BLOCK)
            own[2 + b] = dot(rbuf[hl, 2, rows, :], rbuf[hl, 3, rows, :], TN)
        csend[hl, 0] = (own[0, other, :] + own[1, other, :]).astype(BF16)
        csend[hl, 1] = (own[2, other, :] + own[3, other, :]).astype(BF16)
        c_copy(hl).start()
        own_kv = own[0, mine, :] + own[1, mine, :]
        own_qg = own[2, mine, :] + own[3, mine, :]
        c_copy(hl).wait_recv()
        chip_kv = own_kv + cbuf[hl, 0].astype(F32)
        chip_qg = own_qg + cbuf[hl, 1].astype(F32)
        ysend[hl, 0] = chip_kv.astype(BF16)
        ysend[hl, 1] = chip_qg.astype(BF16)
        for d in (2, 1, 3):
            y_copy(hl, d).start()
        within_block(hl, 0)
        for d in (1, 3, 2):
            y_copy(hl, d).wait_recv()
        row_kv = own[0, mine, :] + own[1, mine, :] + cbuf[hl, 0].astype(F32)
        row_qg = own[2, mine, :] + own[3, mine, :] + cbuf[hl, 1].astype(F32)
        for d in (1, 2, 3):
            source = lax.rem(y + d, NY)
            row_kv = row_kv + ybuf[hl, source, 0].astype(F32)
            row_qg = row_qg + ybuf[hl, source, 1].astype(F32)
        xsend[hl, 0] = row_kv.astype(BF16)
        xsend[hl, 1] = row_qg.astype(BF16)
        for d in (2, 1, 3):
            x_copy(hl, d).start()
        within_block(hl, 1)
        before = jnp.zeros((HALF, 128), F32)
        after = jnp.zeros((HALF, 128), F32)
        for d in (1, 2, 3):
            source = lax.rem(y + d, NY)
            before = before + jnp.where(source < y, ybuf[hl, source, 0].astype(F32), 0.0)
            after = after + jnp.where(source > y, ybuf[hl, source, 1].astype(F32), 0.0)
        for d in (1, 3, 2):
            x_copy(hl, d).wait_recv()
        for d in (1, 2, 3):
            source = lax.rem(x + d, NX)
            got = xbuf[hl, source].astype(F32)
            before = before + jnp.where(source < x, got, 0.0)
            after = after + jnp.where(source > x, got, 0.0)
        own_kv = own[0, mine, :] + own[1, mine, :]
        own_qg = own[2, mine, :] + own[3, mine, :]
        fsend[hl, 0] = (before + jnp.where(core == 0, own_kv, 0.0)).astype(BF16)
        fsend[hl, 1] = (after + jnp.where(core == 1, own_qg, 0.0)).astype(BF16)
        f_copy(hl).start()
        before = before + jnp.where(core == 1, cbuf[hl, 0].astype(F32), 0.0)
        after = after + jnp.where(core == 0, cbuf[hl, 1].astype(F32), 0.0)
        before_used[0, mine, :] = before.astype(BF16)
        before_used[1, mine, :] = (before + own[0, mine, :]).astype(BF16)
        after_used[0, mine, :] = (after + own[3, mine, :]).astype(BF16)
        after_used[1, mine, :] = after.astype(BF16)
        f_copy(hl).wait_recv()
        before = fbuf[hl, 0].astype(F32)
        after = fbuf[hl, 1].astype(F32)
        before_used[0, other, :] = fbuf[hl, 0]
        before_used[1, other, :] = (before + own[0, other, :]).astype(BF16)
        after_used[0, other, :] = (after + own[3, other, :]).astype(BF16)
        after_used[1, other, :] = fbuf[hl, 1]
        for b in range(2):
            rows = pl.ds(b * BLOCK, BLOCK)
            to = pl.ds(b * BLOCK * 4 + hl, BLOCK, stride=4)
            k, v, q, g = (rbuf[hl, a, rows, :] for a in range(4))
            out_ref[0, to, :] = (dot(q, before_used[b], NN) + part[0, rows, :]) * recip_out[rows, :]
            out_ref[1, to, :] = dot(g, before_used[b], NT) + part[1, rows, :]
            out_ref[2, to, :] = dot(v, after_used[b], NT) + part[2, rows, :]
            out_ref[3, to, :] = dot(k, after_used[b], NN) + part[3, rows, :]
        return carry

    lax.fori_loop(0, 4, head, 0)

    def settle(hl, carry):
        for a in range(4):
            for d in FAR_FIRST:
                z_copy(hl, a, d).wait_send()
        c_copy(hl).wait_send()
        f_copy(hl).wait_send()
        for d in (1, 2, 3):
            y_copy(hl, d).wait_send()
            x_copy(hl, d).wait_send()
        return carry

    lax.fori_loop(0, 4, settle, 0)


def exchange(queries, keys_in, values, cotangent):
    flat = [
        pltpu.with_memory_space_constraint(a.reshape(ROWS * 32, 128), pltpu.HBM)
        for a in (queries, keys_in, values, cotangent)
    ]
    dma = pltpu.SemaphoreType.DMA
    return pl.pallas_call(
        exchange_kernel,
        out_shape=jax.ShapeDtypeStruct((4, 4096, 128), F32),
        in_specs=[pl.BlockSpec(memory_space=pl.ANY)] * 4,
        out_specs=pl.BlockSpec(memory_space=pltpu.VMEM),
        scratch_shapes=[
            pltpu.VMEM((4, ROWS * 32, 128), BF16),
            pltpu.VMEM((4, ROWS * 32, 128), F32),
            pltpu.VMEM((4, NZ, 4, ROWS, 128), BF16),
            pltpu.VMEM((4, 4, 1024, 128), BF16),
            pltpu.VMEM((ROWS, 128), F32),
            pltpu.VMEM((1024, 128), F32),
            pltpu.VMEM((4, 128, 128), F32),
            pltpu.VMEM((4, 1024, 128), F32),
            pltpu.VMEM((2, 128, 128), BF16),
            pltpu.VMEM((2, 128, 128), BF16),
            pltpu.VMEM((4, 2, HALF, 128), BF16),
            pltpu.VMEM((4, 2, HALF, 128), BF16),
            pltpu.VMEM((4, 2, HALF, 128), BF16),
            pltpu.VMEM((4, NY, 2, HALF, 128), BF16),
            pltpu.VMEM((4, 2, HALF, 128), BF16),
            pltpu.VMEM((4, NX, HALF, 128), BF16),
            pltpu.VMEM((4, 2, HALF, 128), BF16),
            pltpu.VMEM((4, 2, HALF, 128), BF16),
            dma((4,)), dma((4, 4, NZ)), dma((4, 4, NZ)), dma((4,)),
            dma((4,)), dma((4,)), dma((4, 4)), dma((4, 4)), dma((4, 4)), dma((4, 4)),
            dma((4,)), dma((4,)),
        ],
        compiler_params=pltpu.CompilerParams(
            collective_id=0, has_side_effects=True, vmem_limit_bytes=36 << 20
        ),
        name="exchange",
    )(*flat)


def pack_kernel(wide_ref, *refs):
    outs, narrow, sem = refs[:4], refs[4], refs[5]
    copies = []
    for c in range(4):
        for a in range(4):
            rows = pl.ds(c * 1024, 1024)
            narrow[a, rows, :] = wide_ref[a, rows, :].astype(BF16)
            copy = pltpu.make_async_copy(narrow.at[a, rows, :], outs[a].at[rows, :], sem.at[a, c])
            copy.start()
            copies.append(copy)
    for copy in copies:
        copy.wait()


def pack(wide):
    out = jax.ShapeDtypeStruct((4096, 128), BF16)
    results = pl.pallas_call(
        pack_kernel,
        out_shape=(out,) * 4,
        in_specs=[pl.BlockSpec(memory_space=pltpu.VMEM)],
        out_specs=(pl.BlockSpec(memory_space=pl.ANY),) * 4,
        scratch_shapes=[pltpu.VMEM((4, 4096, 128), BF16), pltpu.SemaphoreType.DMA((4, 4))],
        compiler_params=pltpu.CompilerParams(vmem_limit_bytes=16 << 20),
        name="pack",
    )(wide)
    return tuple(r.reshape(1024, 4, 128) for r in results)


def shards(queries, keys_in, values, cotangent):
    return pack(exchange(queries, keys_in, values, cotangent))


def solution(mesh):
    in_specs = (P(("seq", "head"), None, None),) * 4
    out_specs = (P("seq", "head", None),) * 4
    return jax.shard_map(shards, mesh=mesh, in_specs=in_specs, out_specs=out_specs, check_vma=False)
```

```python
import functools

import jax
import jax.numpy as jnp
from jax import lax
from jax.experimental import pallas as pl
from jax.experimental.pallas import tpu as pltpu
from jax.sharding import PartitionSpec as P

BLOCK = 512
OFFSET = 1048576
MESH = pl.DeviceIdType.MESH
NZ = 8
NX = 4
ROWS = 128
HALF = 64
STRIP = 256
FAR_FIRST = (4, 3, 5, 2, 6, 1, 7)
ROW_ORDER = ((2, 0), (2, 1), (1, 0), (1, 1), (3, 0), (3, 1), (0, 1))
F32 = jnp.float32
BF16 = jnp.bfloat16


def dot(a, b, dims):
    return lax.dot_general(a, b, (dims, ((), ())), preferred_element_type=F32)


NN = ((1,), (0,))
NT = ((1,), (1,))
TN = ((0,), (0,))


def exchange_kernel(
    q_ref, k_ref, v_ref, g_ref, out_ref,
    inb, stg, sbuf, rbuf, recip, recip_out, own, part, state_used,
    half_send, row_buf, total_send, total_buf, pair_send, pair_buf,
    in_sem, s_sem, r_sem, l_sem, hs_sem, hr_sem, ts_sem, tr_sem, ps_sem, pr_sem,
):
    z = lax.axis_index("head")
    seq = lax.axis_index("seq")
    core = lax.rem(seq, 2)
    x = seq // 8
    place = lax.rem(seq, 8)
    row_start = x * 8
    partner = seq + 1 - 2 * core

    def row_peer(d, flip):
        return lax.rem(place - core + 2 * d, 8) + (1 - core if flip else core)

    inputs = (q_ref, g_ref, k_ref, v_ref)

    def load(a):
        return pltpu.make_async_copy(inputs[a], inb.at[a], in_sem.at[a])

    load(0).start()

    barrier = pltpu.get_barrier_semaphore()
    for d in range(1, NZ):
        pl.semaphore_signal(
            barrier, inc=1, device_id={"head": lax.rem(z + d, NZ)}, device_id_type=MESH
        )
    row_peers = [row_start + row_peer(d, flip) for d, flip in ROW_ORDER]
    x_peers = [
        lax.rem(x + d, NX) * 8 + place - core + c
        for d in (2, 1, 3) for c in range(2)
    ]
    for peer in row_peers + x_peers:
        pl.semaphore_signal(barrier, inc=1, device_id={"seq": peer}, device_id_type=MESH)

    first_row = (seq * NZ + z) * ROWS + OFFSET + 1
    position = (first_row + lax.broadcasted_iota(jnp.int32, (ROWS, 128), 0)).astype(F32)
    recip[...] = 1.0 / position

    def head_major(hl, a):
        for dest in range(NZ):
            piece = stg[a, pl.ds(dest * 4 + hl, ROWS, stride=32), :]
            if a == 1:
                piece = piece * recip[...]
            sbuf[hl, dest, a] = piece.astype(BF16)

    here = pl.ds(pl.multiple_of(z * ROWS, ROWS), ROWS)

    def z_copy(hl, st, d):
        dest = lax.rem(z + d, NZ)
        return pltpu.make_async_remote_copy(
            src_ref=sbuf.at[hl, dest, pl.ds(2 * st, 2)],
            dst_ref=rbuf.at[hl, pl.ds(2 * st, 2), here, :],
            send_sem=s_sem,
            recv_sem=r_sem.at[hl, st],
            device_id={"head": dest},
            device_id_type=MESH,
        )

    def local_copy(hl):
        return pltpu.make_async_copy(sbuf.at[hl, z], rbuf.at[hl, :, here, :], l_sem.at[hl])

    load(0).wait()
    for a in range(1, 4):
        load(a).start()
    for hl in range(4):
        for a in range(4):
            if hl == 0:
                if a:
                    load(a).wait()
                stg[a] = inb[a].astype(F32)
            head_major(hl, a)
            if hl == 0 and a == 1:
                pl.semaphore_wait(barrier, 20)
            if a % 2:
                for d in FAR_FIRST:
                    z_copy(hl, a // 2, d).start()
        local_copy(hl).start()

    position = (
        seq * 1024 + OFFSET + 1 + lax.broadcasted_iota(jnp.int32, (1024, 128), 0)
    ).astype(F32)
    recip_out[...] = 1.0 / position

    def half_copy(hl, st, d, flip):
        to = row_peer(d, flip)
        return pltpu.make_async_remote_copy(
            src_ref=half_send.at[hl, st, lax.rem(to, 2)],
            dst_ref=row_buf.at[hl, st, place],
            send_sem=hs_sem,
            recv_sem=hr_sem.at[hl, st],
            device_id={"seq": row_start + to},
            device_id_type=MESH,
        )

    def total_copy(hl, st, d, c):
        return pltpu.make_async_remote_copy(
            src_ref=total_send.at[hl, st],
            dst_ref=total_buf.at[hl, st, x, core],
            send_sem=ts_sem,
            recv_sem=tr_sem.at[hl, st, d - 1],
            device_id={"seq": lax.rem(x + d, NX) * 8 + place - core + c},
            device_id_type=MESH,
        )

    def pair_copy(hl, st):
        return pltpu.make_async_remote_copy(
            src_ref=pair_send.at[hl, st],
            dst_ref=pair_buf.at[hl, st],
            send_sem=ps_sem,
            recv_sem=pr_sem.at[hl, st],
            device_id={"seq": partner},
            device_id_type=MESH,
        )

    def wait_bytes(ref, sem):
        pltpu.make_async_copy(ref, ref, sem).wait()

    def goes(st, d):
        to = lax.rem(x + d, NX)
        return to < x if st == 0 else to > x

    def comes(st, d):
        source = lax.rem(x + NX - d, NX)
        return source > x if st == 0 else source < x

    mine = pl.ds(pl.multiple_of(core * HALF, HALF), HALF)
    other = pl.ds(pl.multiple_of((1 - core) * HALF, HALF), HALF)

    def within_block(hl, b):
        for t in range(2):
            rows = pl.ds(b * BLOCK + t * STRIP, STRIP)
            reach = (t + 1) * STRIP
            seen = pl.ds(b * BLOCK, reach)
            q, g = rbuf[hl, 0, rows, :], rbuf[hl, 1, rows, :]
            k, v = rbuf[hl, 2, seen, :], rbuf[hl, 3, seen, :]
            mask = t * STRIP + lax.broadcasted_iota(
                jnp.int32, (STRIP, reach), 0
            ) >= lax.broadcasted_iota(jnp.int32, (STRIP, reach), 1)
            score = jnp.where(mask, dot(q, k, NT), 0.0).astype(BF16)
            grad_score = jnp.where(mask, dot(g, v, NT), 0.0).astype(BF16)
            part[0, rows, :] = dot(score, v, NN)
            part[1, rows, :] = dot(grad_score, k, NN)
            grad_key = dot(grad_score, q, TN)
            grad_value = dot(score, g, TN)
            if t:
                first = pl.ds(b * BLOCK, STRIP)
                part[2, first, :] += grad_key[:STRIP]
                part[3, first, :] += grad_value[:STRIP]
            part[2, rows, :] = grad_key[t * STRIP :]
            part[3, rows, :] = grad_value[t * STRIP :]

    def own_states(hl, st):
        for b in range(2):
            rows = pl.ds(b * BLOCK, BLOCK)
            own[2 * st + b] = dot(rbuf[hl, 2 * st, rows, :], rbuf[hl, 2 * st + 1, rows, :], TN)
        for c in range(2):
            half = pl.ds(c * HALF, HALF)
            half_send[hl, st, c] = (own[2 * st, half, :] + own[2 * st + 1, half, :]).astype(BF16)
        for d, flip in ROW_ORDER:
            half_copy(hl, st, d, flip).start()

    def row_sums(hl, st):
        wait_bytes(row_buf.at[hl, st, pl.ds(0, 7)], hr_sem.at[hl, st])
        total = own[2 * st, mine, :] + own[2 * st + 1, mine, :]
        first = place - core
        here_sum = jnp.zeros((HALF, 128), F32)
        for d, flip in ROW_ORDER:
            source = row_peer(d, flip)
            got = row_buf[hl, st, source].astype(F32)
            if d:
                outside = source > first + 1 if st == 0 else source < first
                here_sum = here_sum + jnp.where(outside, got, 0.0)
            total = total + got
        total_send[hl, st] = total.astype(BF16)
        for d in (2, 1, 3):
            @pl.when(goes(st, d))
            def _():
                for c in range(2):
                    total_copy(hl, st, d, c).start()
        lone = own[2 * st, mine, :] + own[2 * st + 1, mine, :]
        pair = row_buf[hl, st, row_peer(0, 1)].astype(F32)
        takes = core == st
        pair_send[hl, st] = (here_sum + jnp.where(takes, 0.0, lone)).astype(BF16)
        pair_copy(hl, st).start()
        own[4 + st, mine, :] = here_sum + jnp.where(takes, pair, 0.0)

    def finish_state(hl, st):
        wait_bytes(pair_buf.at[hl, st], pr_sem.at[hl, st])
        own[4 + st, other, :] = pair_buf[hl, st].astype(F32)
        for d in (1, 3, 2):
            @pl.when(comes(st, d))
            def _():
                source = lax.rem(x + NX - d, NX)
                wait_bytes(total_buf.at[hl, st, source], tr_sem.at[hl, st, d - 1])
                for c in range(2):
                    half = pl.ds(c * HALF, HALF)
                    own[4 + st, half, :] += total_buf[hl, st, source, c].astype(F32)
        outer = own[4 + st]
        state_used[st, 1 - st] = outer.astype(BF16)
        state_used[st, st] = (outer + own[1 + st]).astype(BF16)

    def wait_rows(hl, st):
        wait_bytes(rbuf.at[hl, pl.ds(0, 2), pl.ds(0, 7 * ROWS)], r_sem.at[hl, st])

    def head(hl, carry):
        wait_rows(hl, 0)
        local_copy(hl).wait()
        own_states(hl, 0)
        row_sums(hl, 0)
        finish_state(hl, 0)
        wait_rows(hl, 1)
        own_states(hl, 1)
        within_block(hl, 0)
        within_block(hl, 1)
        row_sums(hl, 1)
        for b in range(2):
            rows = pl.ds(b * BLOCK, BLOCK)
            to = pl.ds(b * BLOCK * 4 + hl, BLOCK, stride=4)
            k, v = rbuf[hl, 2, rows, :], rbuf[hl, 3, rows, :]
            state = state_used[0, b]
            out_ref[2, to, :] = dot(v, state, NT) + part[2, rows, :]
            out_ref[3, to, :] = dot(k, state, NN) + part[3, rows, :]
        finish_state(hl, 1)
        for b in range(2):
            rows = pl.ds(b * BLOCK, BLOCK)
            to = pl.ds(b * BLOCK * 4 + hl, BLOCK, stride=4)
            q, g = rbuf[hl, 0, rows, :], rbuf[hl, 1, rows, :]
            state = state_used[1, b]
            out_ref[0, to, :] = (dot(q, state, NN) + part[0, rows, :]) * recip_out[rows, :]
            out_ref[1, to, :] = dot(g, state, NT) + part[1, rows, :]
        return carry

    lax.fori_loop(0, 4, head, 0)

    wait_bytes(sbuf.at[:, pl.ds(0, 7)], s_sem)
    wait_bytes(row_buf.at[:, :, pl.ds(0, 7)], hs_sem)
    wait_bytes(total_buf.at[:, 0, pl.ds(0, 3)], ts_sem)
    wait_bytes(pair_buf, ps_sem)


def exchange(queries, keys_in, values, cotangent):
    flat = [
        pltpu.with_memory_space_constraint(a.reshape(ROWS * 32, 128), pltpu.HBM)
        for a in (queries, keys_in, values, cotangent)
    ]
    dma = pltpu.SemaphoreType.DMA
    return pl.pallas_call(
        exchange_kernel,
        out_shape=jax.ShapeDtypeStruct((4, 4096, 128), F32),
        in_specs=[pl.BlockSpec(memory_space=pl.ANY)] * 4,
        out_specs=pl.BlockSpec(memory_space=pltpu.VMEM),
        scratch_shapes=[
            pltpu.VMEM((4, ROWS * 32, 128), BF16),
            pltpu.VMEM((4, ROWS * 32, 128), F32),
            pltpu.VMEM((4, NZ, 4, ROWS, 128), BF16),
            pltpu.VMEM((4, 4, 1024, 128), BF16),
            pltpu.VMEM((ROWS, 128), F32),
            pltpu.VMEM((1024, 128), F32),
            pltpu.VMEM((6, 128, 128), F32),
            pltpu.VMEM((4, 1024, 128), F32),
            pltpu.VMEM((2, 2, 128, 128), BF16),
            pltpu.VMEM((4, 2, 2, HALF, 128), BF16),
            pltpu.VMEM((4, 2, 8, HALF, 128), BF16),
            pltpu.VMEM((4, 2, HALF, 128), BF16),
            pltpu.VMEM((4, 2, NX, 2, HALF, 128), BF16),
            pltpu.VMEM((4, 2, HALF, 128), BF16),
            pltpu.VMEM((4, 2, HALF, 128), BF16),
            dma((4,)), dma, dma((4, 2)), dma((4,)),
            dma, dma((4, 2)), dma, dma((4, 2, 3)), dma, dma((4, 2)),
        ],
        compiler_params=pltpu.CompilerParams(
            collective_id=0, has_side_effects=True, vmem_limit_bytes=36 << 20
        ),
        name="exchange",
    )(*flat)


def pack_kernel(wide_ref, *refs):
    outs, narrow, sem = refs[:4], refs[4], refs[5]
    copies = []
    for c in range(4):
        for a in range(4):
            rows = pl.ds(c * 1024, 1024)
            narrow[a, rows, :] = wide_ref[a, rows, :].astype(BF16)
            copy = pltpu.make_async_copy(narrow.at[a, rows, :], outs[a].at[rows, :], sem.at[a, c])
            copy.start()
            copies.append(copy)
    for copy in copies:
        copy.wait()


def pack(wide):
    out = jax.ShapeDtypeStruct((4096, 128), BF16)
    results = pl.pallas_call(
        pack_kernel,
        out_shape=(out,) * 4,
        in_specs=[pl.BlockSpec(memory_space=pltpu.VMEM)],
        out_specs=(pl.BlockSpec(memory_space=pl.ANY),) * 4,
        scratch_shapes=[pltpu.VMEM((4, 4096, 128), BF16), pltpu.SemaphoreType.DMA((4, 4))],
        compiler_params=pltpu.CompilerParams(vmem_limit_bytes=16 << 20),
        name="pack",
    )(wide)
    return tuple(r.reshape(1024, 4, 128) for r in results)


def shards(queries, keys_in, values, cotangent):
    return pack(exchange(queries, keys_in, values, cotangent))


def solution(mesh):
    in_specs = (P(("seq", "head"), None, None),) * 4
    out_specs = (P("seq", "head", None),) * 4
    return jax.shard_map(shards, mesh=mesh, in_specs=in_specs, out_specs=out_specs, check_vma=False)
```

```python
import functools

import jax
import jax.numpy as jnp
from jax import lax
from jax.experimental import pallas as pl
from jax.experimental.pallas import tpu as pltpu
from jax.sharding import PartitionSpec as P

BLOCK = 512
OFFSET = 1048576
MESH = pl.DeviceIdType.MESH
NZ = 8
NX = 4
ROWS = 128
HALF = 64
STRIP = 256
FAR_FIRST = (4, 3, 5, 2, 6, 1, 7)
PLANES = (0, 1, 2, 3, 7, 4, 6, 5)
ROW_ORDER = ((2, 0), (2, 1), (1, 0), (1, 1), (3, 0), (3, 1), (0, 1))
F32 = jnp.float32
BF16 = jnp.bfloat16


def dot(a, b, dims):
    return lax.dot_general(a, b, (dims, ((), ())), preferred_element_type=F32)


NN = ((1,), (0,))
NT = ((1,), (1,))
TN = ((0,), (0,))


def exchange_kernel(
    q_ref, k_ref, v_ref, g_ref, out_ref,
    inb, stg, sbuf, rbuf, recip, recip_out, own, part, state_used,
    half_send, row_buf, total_send, total_buf, pair_send, pair_buf,
    in_sem, s_sem, r_sem, l_sem, hs_sem, hr_sem, ts_sem, tr_sem, ps_sem, pr_sem,
):
    z = lax.axis_index("head")
    seq = lax.axis_index("seq")
    core = lax.rem(seq, 2)
    x = seq // 8
    place = lax.rem(seq, 8)
    row_start = x * 8
    partner = seq + 1 - 2 * core

    def row_peer(d, flip):
        return lax.rem(place - core + 2 * d, 8) + (1 - core if flip else core)

    inputs = (q_ref, g_ref, k_ref, v_ref)

    def load(a):
        return pltpu.make_async_copy(inputs[a], inb.at[a], in_sem.at[a])

    load(0).start()

    barrier = pltpu.get_barrier_semaphore()
    for d in range(1, NZ):
        pl.semaphore_signal(
            barrier, inc=1, device_id={"head": lax.rem(z + d, NZ)}, device_id_type=MESH
        )
    row_peers = [row_start + row_peer(d, flip) for d, flip in ROW_ORDER]
    x_peers = [
        lax.rem(x + d, NX) * 8 + place - core + c
        for d in (2, 1, 3) for c in range(2)
    ]
    for peer in row_peers + x_peers:
        pl.semaphore_signal(barrier, inc=1, device_id={"seq": peer}, device_id_type=MESH)

    first_row = (seq * NZ + z) * ROWS + OFFSET + 1
    position = (first_row + lax.broadcasted_iota(jnp.int32, (ROWS, 128), 0)).astype(F32)
    recip[...] = 1.0 / position

    def head_major(hl, a):
        for dest in range(NZ):
            piece = stg[a, pl.ds(dest * 4 + hl, ROWS, stride=32), :]
            if a == 1:
                piece = piece * recip[...]
            sbuf[hl, dest, a] = piece.astype(BF16)

    here = pl.ds(pl.multiple_of(z * ROWS, ROWS), ROWS)

    def z_copy(hl, st, d):
        dest = lax.rem(z + d, NZ)
        return pltpu.make_async_remote_copy(
            src_ref=sbuf.at[hl, dest, pl.ds(2 * st, 2)],
            dst_ref=rbuf.at[hl, pl.ds(2 * st, 2), here, :],
            send_sem=s_sem,
            recv_sem=r_sem.at[hl, st],
            device_id={"head": dest},
            device_id_type=MESH,
        )

    def local_copy(hl):
        return pltpu.make_async_copy(sbuf.at[hl, z], rbuf.at[hl, :, here, :], l_sem.at[hl])

    load(0).wait()
    for a in range(1, 4):
        load(a).start()
    for hl in range(4):
        for a in range(4):
            if hl == 0:
                if a:
                    load(a).wait()
                stg[a] = inb[a].astype(F32)
            head_major(hl, a)
            if hl == 0 and a == 1:
                pl.semaphore_wait(barrier, 20)
            if a % 2:
                if hl < 3 or a < 1:
                    for d in FAR_FIRST:
                        z_copy(hl, a // 2, d).start()
                else:
                    for dest in PLANES:
                        @pl.when(dest != z)
                        def _():
                            z_copy(hl, a // 2, lax.rem(dest + NZ - z, NZ)).start()
        local_copy(hl).start()

    position = (
        seq * 1024 + OFFSET + 1 + lax.broadcasted_iota(jnp.int32, (1024, 128), 0)
    ).astype(F32)
    recip_out[...] = 1.0 / position

    def half_copy(hl, st, d, flip):
        to = row_peer(d, flip)
        return pltpu.make_async_remote_copy(
            src_ref=half_send.at[hl, st, lax.rem(to, 2)],
            dst_ref=row_buf.at[hl, st, place],
            send_sem=hs_sem,
            recv_sem=hr_sem.at[hl, st],
            device_id={"seq": row_start + to},
            device_id_type=MESH,
        )

    def total_copy(hl, st, d, c):
        return pltpu.make_async_remote_copy(
            src_ref=total_send.at[hl, st],
            dst_ref=total_buf.at[hl, st, x, core],
            send_sem=ts_sem,
            recv_sem=tr_sem.at[hl, st, d - 1],
            device_id={"seq": lax.rem(x + d, NX) * 8 + place - core + c},
            device_id_type=MESH,
        )

    def pair_copy(hl, st):
        return pltpu.make_async_remote_copy(
            src_ref=pair_send.at[hl, st],
            dst_ref=pair_buf.at[hl, st],
            send_sem=ps_sem,
            recv_sem=pr_sem.at[hl, st],
            device_id={"seq": partner},
            device_id_type=MESH,
        )

    def wait_bytes(ref, sem):
        pltpu.make_async_copy(ref, ref, sem).wait()

    def goes(st, d):
        to = lax.rem(x + d, NX)
        return to < x if st == 0 else to > x

    def comes(st, d):
        source = lax.rem(x + NX - d, NX)
        return source > x if st == 0 else source < x

    mine = pl.ds(pl.multiple_of(core * HALF, HALF), HALF)
    other = pl.ds(pl.multiple_of((1 - core) * HALF, HALF), HALF)

    def within_block(hl, b):
        for t in range(2):
            rows = pl.ds(b * BLOCK + t * STRIP, STRIP)
            reach = (t + 1) * STRIP
            seen = pl.ds(b * BLOCK, reach)
            q, g = rbuf[hl, 0, rows, :], rbuf[hl, 1, rows, :]
            k, v = rbuf[hl, 2, seen, :], rbuf[hl, 3, seen, :]
            mask = t * STRIP + lax.broadcasted_iota(
                jnp.int32, (STRIP, reach), 0
            ) >= lax.broadcasted_iota(jnp.int32, (STRIP, reach), 1)
            score = jnp.where(mask, dot(q, k, NT), 0.0).astype(BF16)
            grad_score = jnp.where(mask, dot(g, v, NT), 0.0).astype(BF16)
            part[0, rows, :] = dot(score, v, NN)
            part[1, rows, :] = dot(grad_score, k, NN)
            grad_key = dot(grad_score, q, TN)
            grad_value = dot(score, g, TN)
            if t:
                first = pl.ds(b * BLOCK, STRIP)
                part[2, first, :] += grad_key[:STRIP]
                part[3, first, :] += grad_value[:STRIP]
            part[2, rows, :] = grad_key[t * STRIP :]
            part[3, rows, :] = grad_value[t * STRIP :]

    def own_states(hl, st):
        for b in range(2):
            rows = pl.ds(b * BLOCK, BLOCK)
            own[2 * st + b] = dot(rbuf[hl, 2 * st, rows, :], rbuf[hl, 2 * st + 1, rows, :], TN)
        for c in range(2):
            half = pl.ds(c * HALF, HALF)
            half_send[hl, st, c] = (own[2 * st, half, :] + own[2 * st + 1, half, :]).astype(BF16)
        for d, flip in ROW_ORDER:
            half_copy(hl, st, d, flip).start()

    def row_sums(hl, st):
        wait_bytes(row_buf.at[hl, st, pl.ds(0, 7)], hr_sem.at[hl, st])
        total = own[2 * st, mine, :] + own[2 * st + 1, mine, :]
        first = place - core
        here_sum = jnp.zeros((HALF, 128), F32)
        for d, flip in ROW_ORDER:
            source = row_peer(d, flip)
            got = row_buf[hl, st, source].astype(F32)
            if d:
                outside = source > first + 1 if st == 0 else source < first
                here_sum = here_sum + jnp.where(outside, got, 0.0)
            total = total + got
        total_send[hl, st] = total.astype(BF16)
        for d in (2, 1, 3):
            @pl.when(goes(st, d))
            def _():
                for c in range(2):
                    total_copy(hl, st, d, c).start()
        lone = own[2 * st, mine, :] + own[2 * st + 1, mine, :]
        pair = row_buf[hl, st, row_peer(0, 1)].astype(F32)
        takes = core == st
        pair_send[hl, st] = (here_sum + jnp.where(takes, 0.0, lone)).astype(BF16)
        pair_copy(hl, st).start()
        own[4 + st, mine, :] = here_sum + jnp.where(takes, pair, 0.0)

    def finish_state(hl, st):
        wait_bytes(pair_buf.at[hl, st], pr_sem.at[hl, st])
        own[4 + st, other, :] = pair_buf[hl, st].astype(F32)
        for d in (1, 3, 2):
            @pl.when(comes(st, d))
            def _():
                source = lax.rem(x + NX - d, NX)
                wait_bytes(total_buf.at[hl, st, source], tr_sem.at[hl, st, d - 1])
                for c in range(2):
                    half = pl.ds(c * HALF, HALF)
                    own[4 + st, half, :] += total_buf[hl, st, source, c].astype(F32)
        outer = own[4 + st]
        state_used[st, 1 - st] = outer.astype(BF16)
        state_used[st, st] = (outer + own[1 + st]).astype(BF16)

    def wait_rows(hl, st):
        wait_bytes(rbuf.at[hl, pl.ds(0, 2), pl.ds(0, 7 * ROWS)], r_sem.at[hl, st])

    def head(hl, carry):
        wait_rows(hl, 0)
        local_copy(hl).wait()
        own_states(hl, 0)
        row_sums(hl, 0)
        finish_state(hl, 0)
        wait_rows(hl, 1)
        own_states(hl, 1)
        within_block(hl, 0)
        within_block(hl, 1)
        row_sums(hl, 1)
        for b in range(2):
            rows = pl.ds(b * BLOCK, BLOCK)
            to = pl.ds(b * BLOCK * 4 + hl, BLOCK, stride=4)
            k, v = rbuf[hl, 2, rows, :], rbuf[hl, 3, rows, :]
            state = state_used[0, b]
            out_ref[2, to, :] = dot(v, state, NT) + part[2, rows, :]
            out_ref[3, to, :] = dot(k, state, NN) + part[3, rows, :]
        finish_state(hl, 1)
        for b in range(2):
            rows = pl.ds(b * BLOCK, BLOCK)
            to = pl.ds(b * BLOCK * 4 + hl, BLOCK, stride=4)
            q, g = rbuf[hl, 0, rows, :], rbuf[hl, 1, rows, :]
            state = state_used[1, b]
            out_ref[0, to, :] = (dot(q, state, NN) + part[0, rows, :]) * recip_out[rows, :]
            out_ref[1, to, :] = dot(g, state, NT) + part[1, rows, :]
        return carry

    lax.fori_loop(0, 4, head, 0)

    wait_bytes(sbuf.at[:, pl.ds(0, 7)], s_sem)
    wait_bytes(row_buf.at[:, :, pl.ds(0, 7)], hs_sem)
    wait_bytes(total_buf.at[:, 0, pl.ds(0, 3)], ts_sem)
    wait_bytes(pair_buf, ps_sem)


def exchange(queries, keys_in, values, cotangent):
    flat = [
        pltpu.with_memory_space_constraint(a.reshape(ROWS * 32, 128), pltpu.HBM)
        for a in (queries, keys_in, values, cotangent)
    ]
    dma = pltpu.SemaphoreType.DMA
    return pl.pallas_call(
        exchange_kernel,
        out_shape=jax.ShapeDtypeStruct((4, 4096, 128), F32),
        in_specs=[pl.BlockSpec(memory_space=pl.ANY)] * 4,
        out_specs=pl.BlockSpec(memory_space=pltpu.VMEM),
        scratch_shapes=[
            pltpu.VMEM((4, ROWS * 32, 128), BF16),
            pltpu.VMEM((4, ROWS * 32, 128), F32),
            pltpu.VMEM((4, NZ, 4, ROWS, 128), BF16),
            pltpu.VMEM((4, 4, 1024, 128), BF16),
            pltpu.VMEM((ROWS, 128), F32),
            pltpu.VMEM((1024, 128), F32),
            pltpu.VMEM((6, 128, 128), F32),
            pltpu.VMEM((4, 1024, 128), F32),
            pltpu.VMEM((2, 2, 128, 128), BF16),
            pltpu.VMEM((4, 2, 2, HALF, 128), BF16),
            pltpu.VMEM((4, 2, 8, HALF, 128), BF16),
            pltpu.VMEM((4, 2, HALF, 128), BF16),
            pltpu.VMEM((4, 2, NX, 2, HALF, 128), BF16),
            pltpu.VMEM((4, 2, HALF, 128), BF16),
            pltpu.VMEM((4, 2, HALF, 128), BF16),
            dma((4,)), dma, dma((4, 2)), dma((4,)),
            dma, dma((4, 2)), dma, dma((4, 2, 3)), dma, dma((4, 2)),
        ],
        compiler_params=pltpu.CompilerParams(
            collective_id=0, has_side_effects=True, vmem_limit_bytes=36 << 20
        ),
        name="exchange",
    )(*flat)


def pack_kernel(wide_ref, *refs):
    outs, narrow, sem = refs[:4], refs[4], refs[5]
    copies = []
    for c in range(4):
        for a in range(4):
            rows = pl.ds(c * 1024, 1024)
            narrow[a, rows, :] = wide_ref[a, rows, :].astype(BF16)
            copy = pltpu.make_async_copy(narrow.at[a, rows, :], outs[a].at[rows, :], sem.at[a, c])
            copy.start()
            copies.append(copy)
    for copy in copies:
        copy.wait()


def pack(wide):
    out = jax.ShapeDtypeStruct((4096, 128), BF16)
    results = pl.pallas_call(
        pack_kernel,
        out_shape=(out,) * 4,
        in_specs=[pl.BlockSpec(memory_space=pltpu.VMEM)],
        out_specs=(pl.BlockSpec(memory_space=pl.ANY),) * 4,
        scratch_shapes=[pltpu.VMEM((4, 4096, 128), BF16), pltpu.SemaphoreType.DMA((4, 4))],
        compiler_params=pltpu.CompilerParams(vmem_limit_bytes=16 << 20),
        name="pack",
    )(wide)
    return tuple(r.reshape(1024, 4, 128) for r in results)


def shards(queries, keys_in, values, cotangent):
    return pack(exchange(queries, keys_in, values, cotangent))


def solution(mesh):
    in_specs = (P(("seq", "head"), None, None),) * 4
    out_specs = (P("seq", "head", None),) * 4
    return jax.shard_map(shards, mesh=mesh, in_specs=in_specs, out_specs=out_specs, check_vma=False)
```

```python
import functools

import jax
import jax.numpy as jnp
from jax import lax
from jax.experimental import pallas as pl
from jax.experimental.pallas import tpu as pltpu
from jax.sharding import PartitionSpec as P

BLOCK = 512
OFFSET = 1048576
MESH = pl.DeviceIdType.MESH
NZ = 8
NX = 4
ROWS = 128
HALF = 64
STRIP = 256
FAR_FIRST = (4, 3, 5, 2, 6, 1, 7)
PLANES = (0, 1, 2, 3, 7, 4, 6, 5)
ROW_ORDER = ((2, 0), (2, 1), (1, 0), (1, 1), (3, 0), (3, 1), (0, 1))
F32 = jnp.float32
BF16 = jnp.bfloat16


def dot(a, b, dims):
    return lax.dot_general(a, b, (dims, ((), ())), preferred_element_type=F32)


NN = ((1,), (0,))
NT = ((1,), (1,))
TN = ((0,), (0,))


def exchange_kernel(
    q_ref, k_ref, v_ref, g_ref, out_ref,
    inb, stg, sbuf, rbuf, recip, recip_out, own, part, state_used,
    half_send, row_buf, total_send, total_buf, pair_send, pair_buf,
    in_sem, s_sem, r_sem, l_sem, hs_sem, hr_sem, ts_sem, tr_sem, ps_sem, pr_sem,
):
    z = lax.axis_index("head")
    seq = lax.axis_index("seq")
    core = lax.rem(seq, 2)
    x = seq // 8
    place = lax.rem(seq, 8)
    row_start = x * 8
    partner = seq + 1 - 2 * core

    def row_peer(d, flip):
        return lax.rem(place - core + 2 * d, 8) + (1 - core if flip else core)

    inputs = (q_ref, g_ref, k_ref, v_ref)

    def load(a):
        return pltpu.make_async_copy(inputs[a], inb.at[a], in_sem.at[a])

    load(0).start()

    barrier = pltpu.get_barrier_semaphore()
    for d in range(1, NZ):
        pl.semaphore_signal(
            barrier, inc=1, device_id={"head": lax.rem(z + d, NZ)}, device_id_type=MESH
        )
    row_peers = [row_start + row_peer(d, flip) for d, flip in ROW_ORDER]
    x_peers = [
        lax.rem(x + d, NX) * 8 + place - core + c
        for d in (2, 1, 3) for c in range(2)
    ]
    for peer in row_peers + x_peers:
        pl.semaphore_signal(barrier, inc=1, device_id={"seq": peer}, device_id_type=MESH)

    first_row = (seq * NZ + z) * ROWS + OFFSET + 1
    position = (first_row + lax.broadcasted_iota(jnp.int32, (ROWS, 128), 0)).astype(F32)
    recip[...] = 1.0 / position

    def head_major(hl, a):
        for dest in range(NZ):
            piece = stg[a, pl.ds(dest * 4 + hl, ROWS, stride=32), :]
            if a == 1:
                piece = piece * recip[...]
            sbuf[hl, dest, a] = piece.astype(BF16)

    here = pl.ds(pl.multiple_of(z * ROWS, ROWS), ROWS)

    def z_copy(hl, st, d):
        dest = lax.rem(z + d, NZ)
        return pltpu.make_async_remote_copy(
            src_ref=sbuf.at[hl, dest, pl.ds(2 * st, 2)],
            dst_ref=rbuf.at[hl, pl.ds(2 * st, 2), here, :],
            send_sem=s_sem,
            recv_sem=r_sem.at[hl, st],
            device_id={"head": dest},
            device_id_type=MESH,
        )

    def local_copy(hl):
        return pltpu.make_async_copy(sbuf.at[hl, z], rbuf.at[hl, :, here, :], l_sem.at[hl])

    load(0).wait()
    for a in range(1, 4):
        load(a).start()
    for hl in range(4):
        for a in range(4):
            if hl == 0:
                if a:
                    load(a).wait()
                stg[a] = inb[a].astype(F32)
            head_major(hl, a)
            if hl == 0 and a == 1:
                pl.semaphore_wait(barrier, 20)
            if a % 2:
                if hl < 3 or a < 1:
                    for d in FAR_FIRST:
                        z_copy(hl, a // 2, d).start()
                else:
                    for dest in PLANES:
                        @pl.when(dest != z)
                        def _():
                            z_copy(hl, a // 2, lax.rem(dest + NZ - z, NZ)).start()
        local_copy(hl).start()

    position = (
        seq * 1024 + OFFSET + 1 + lax.broadcasted_iota(jnp.int32, (1024, 128), 0)
    ).astype(F32)
    recip_out[...] = 1.0 / position

    def half_copy(hl, st, d, flip):
        to = row_peer(d, flip)
        return pltpu.make_async_remote_copy(
            src_ref=half_send.at[hl, st, lax.rem(to, 2)],
            dst_ref=row_buf.at[hl, st, place],
            send_sem=hs_sem,
            recv_sem=hr_sem.at[hl, st],
            device_id={"seq": row_start + to},
            device_id_type=MESH,
        )

    def total_copy(hl, st, d, c):
        return pltpu.make_async_remote_copy(
            src_ref=total_send.at[hl, st],
            dst_ref=total_buf.at[hl, st, x, core],
            send_sem=ts_sem,
            recv_sem=tr_sem.at[hl, st, d - 1],
            device_id={"seq": lax.rem(x + d, NX) * 8 + place - core + c},
            device_id_type=MESH,
        )

    def pair_copy(hl, st):
        return pltpu.make_async_remote_copy(
            src_ref=pair_send.at[hl, st],
            dst_ref=pair_buf.at[hl, st],
            send_sem=ps_sem,
            recv_sem=pr_sem.at[hl, st],
            device_id={"seq": partner},
            device_id_type=MESH,
        )

    def wait_bytes(ref, sem):
        pltpu.make_async_copy(ref, ref, sem).wait()

    def goes(st, d):
        to = lax.rem(x + d, NX)
        return to < x if st == 0 else to > x

    def comes(st, d):
        source = lax.rem(x + NX - d, NX)
        return source > x if st == 0 else source < x

    mine = pl.ds(pl.multiple_of(core * HALF, HALF), HALF)
    other = pl.ds(pl.multiple_of((1 - core) * HALF, HALF), HALF)

    def within_block(hl, b):
        for t in range(2):
            rows = pl.ds(b * BLOCK + t * STRIP, STRIP)
            reach = (t + 1) * STRIP
            seen = pl.ds(b * BLOCK, reach)
            q, g = rbuf[hl, 0, rows, :], rbuf[hl, 1, rows, :]
            k, v = rbuf[hl, 2, seen, :], rbuf[hl, 3, seen, :]
            mask = t * STRIP + lax.broadcasted_iota(
                jnp.int32, (STRIP, reach), 0
            ) >= lax.broadcasted_iota(jnp.int32, (STRIP, reach), 1)
            score = jnp.where(mask, dot(q, k, NT), 0.0).astype(BF16)
            grad_score = jnp.where(mask, dot(g, v, NT), 0.0).astype(BF16)
            part[0, rows, :] = dot(score, v, NN)
            part[1, rows, :] = dot(grad_score, k, NN)
            grad_key = dot(grad_score, q, TN)
            grad_value = dot(score, g, TN)
            if t:
                first = pl.ds(b * BLOCK, STRIP)
                part[2, first, :] += grad_key[:STRIP]
                part[3, first, :] += grad_value[:STRIP]
            part[2, rows, :] = grad_key[t * STRIP :]
            part[3, rows, :] = grad_value[t * STRIP :]

    def own_states(hl, st):
        for b in range(2):
            rows = pl.ds(b * BLOCK, BLOCK)
            own[2 * st + b] = dot(rbuf[hl, 2 * st, rows, :], rbuf[hl, 2 * st + 1, rows, :], TN)
        for c in range(2):
            half = pl.ds(c * HALF, HALF)
            half_send[hl, st, c] = (own[2 * st, half, :] + own[2 * st + 1, half, :]).astype(BF16)
        for d, flip in ROW_ORDER:
            half_copy(hl, st, d, flip).start()

    def row_sums(hl, st):
        wait_bytes(row_buf.at[hl, st, pl.ds(0, 7)], hr_sem.at[hl, st])
        total = own[2 * st, mine, :] + own[2 * st + 1, mine, :]
        first = place - core
        here_sum = jnp.zeros((HALF, 128), F32)
        for d, flip in ROW_ORDER:
            source = row_peer(d, flip)
            got = row_buf[hl, st, source].astype(F32)
            if d:
                outside = source > first + 1 if st == 0 else source < first
                here_sum = here_sum + jnp.where(outside, got, 0.0)
            total = total + got
        total_send[hl, st] = total.astype(BF16)
        for d in (2, 1, 3):
            @pl.when(goes(st, d))
            def _():
                for c in range(2):
                    total_copy(hl, st, d, c).start()
        lone = own[2 * st, mine, :] + own[2 * st + 1, mine, :]
        pair = row_buf[hl, st, row_peer(0, 1)].astype(F32)
        takes = core == st
        pair_send[hl, st] = (here_sum + jnp.where(takes, 0.0, lone)).astype(BF16)
        pair_copy(hl, st).start()
        own[4 + st, mine, :] = here_sum + jnp.where(takes, pair, 0.0)

    def finish_state(hl, st):
        wait_bytes(pair_buf.at[hl, st], pr_sem.at[hl, st])
        own[4 + st, other, :] = pair_buf[hl, st].astype(F32)
        for d in (1, 3, 2):
            @pl.when(comes(st, d))
            def _():
                source = lax.rem(x + NX - d, NX)
                wait_bytes(total_buf.at[hl, st, source], tr_sem.at[hl, st, d - 1])
                for c in range(2):
                    half = pl.ds(c * HALF, HALF)
                    own[4 + st, half, :] += total_buf[hl, st, source, c].astype(F32)
        outer = own[4 + st]
        state_used[st, 1 - st] = outer.astype(BF16)
        state_used[st, st] = (outer + own[1 + st]).astype(BF16)

    def wait_rows(hl, st):
        wait_bytes(rbuf.at[hl, pl.ds(0, 2), pl.ds(0, 7 * ROWS)], r_sem.at[hl, st])

    def head(hl, carry):
        wait_rows(hl, 0)
        local_copy(hl).wait()
        own_states(hl, 0)
        row_sums(hl, 0)
        finish_state(hl, 0)
        wait_rows(hl, 1)
        own_states(hl, 1)
        within_block(hl, 0)
        row_sums(hl, 1)
        within_block(hl, 1)
        for b in range(2):
            rows = pl.ds(b * BLOCK, BLOCK)
            to = pl.ds(b * BLOCK * 4 + hl, BLOCK, stride=4)
            k, v = rbuf[hl, 2, rows, :], rbuf[hl, 3, rows, :]
            state = state_used[0, b]
            out_ref[2, to, :] = dot(v, state, NT) + part[2, rows, :]
            out_ref[3, to, :] = dot(k, state, NN) + part[3, rows, :]
        finish_state(hl, 1)
        for b in range(2):
            rows = pl.ds(b * BLOCK, BLOCK)
            to = pl.ds(b * BLOCK * 4 + hl, BLOCK, stride=4)
            q, g = rbuf[hl, 0, rows, :], rbuf[hl, 1, rows, :]
            state = state_used[1, b]
            out_ref[0, to, :] = (dot(q, state, NN) + part[0, rows, :]) * recip_out[rows, :]
            out_ref[1, to, :] = dot(g, state, NT) + part[1, rows, :]
        return carry

    lax.fori_loop(0, 4, head, 0)

    wait_bytes(sbuf.at[:, pl.ds(0, 7)], s_sem)
    wait_bytes(row_buf.at[:, :, pl.ds(0, 7)], hs_sem)
    wait_bytes(total_buf.at[:, 0, pl.ds(0, 3)], ts_sem)
    wait_bytes(pair_buf, ps_sem)


def exchange(queries, keys_in, values, cotangent):
    flat = [
        pltpu.with_memory_space_constraint(a.reshape(ROWS * 32, 128), pltpu.HBM)
        for a in (queries, keys_in, values, cotangent)
    ]
    dma = pltpu.SemaphoreType.DMA
    return pl.pallas_call(
        exchange_kernel,
        out_shape=jax.ShapeDtypeStruct((4, 4096, 128), F32),
        in_specs=[pl.BlockSpec(memory_space=pl.ANY)] * 4,
        out_specs=pl.BlockSpec(memory_space=pltpu.VMEM),
        scratch_shapes=[
            pltpu.VMEM((4, ROWS * 32, 128), BF16),
            pltpu.VMEM((4, ROWS * 32, 128), F32),
            pltpu.VMEM((4, NZ, 4, ROWS, 128), BF16),
            pltpu.VMEM((4, 4, 1024, 128), BF16),
            pltpu.VMEM((ROWS, 128), F32),
            pltpu.VMEM((1024, 128), F32),
            pltpu.VMEM((6, 128, 128), F32),
            pltpu.VMEM((4, 1024, 128), F32),
            pltpu.VMEM((2, 2, 128, 128), BF16),
            pltpu.VMEM((4, 2, 2, HALF, 128), BF16),
            pltpu.VMEM((4, 2, 8, HALF, 128), BF16),
            pltpu.VMEM((4, 2, HALF, 128), BF16),
            pltpu.VMEM((4, 2, NX, 2, HALF, 128), BF16),
            pltpu.VMEM((4, 2, HALF, 128), BF16),
            pltpu.VMEM((4, 2, HALF, 128), BF16),
            dma((4,)), dma, dma((4, 2)), dma((4,)),
            dma, dma((4, 2)), dma, dma((4, 2, 3)), dma, dma((4, 2)),
        ],
        compiler_params=pltpu.CompilerParams(
            collective_id=0, has_side_effects=True, vmem_limit_bytes=36 << 20
        ),
        name="exchange",
    )(*flat)


def pack_kernel(wide_ref, *refs):
    outs, narrow, sem = refs[:4], refs[4], refs[5]
    copies = []
    for c in range(4):
        for a in range(4):
            rows = pl.ds(c * 1024, 1024)
            narrow[a, rows, :] = wide_ref[a, rows, :].astype(BF16)
            copy = pltpu.make_async_copy(narrow.at[a, rows, :], outs[a].at[rows, :], sem.at[a, c])
            copy.start()
            copies.append(copy)
    for copy in copies:
        copy.wait()


def pack(wide):
    out = jax.ShapeDtypeStruct((4096, 128), BF16)
    results = pl.pallas_call(
        pack_kernel,
        out_shape=(out,) * 4,
        in_specs=[pl.BlockSpec(memory_space=pltpu.VMEM)],
        out_specs=(pl.BlockSpec(memory_space=pl.ANY),) * 4,
        scratch_shapes=[pltpu.VMEM((4, 4096, 128), BF16), pltpu.SemaphoreType.DMA((4, 4))],
        compiler_params=pltpu.CompilerParams(vmem_limit_bytes=16 << 20),
        name="pack",
    )(wide)
    return tuple(r.reshape(1024, 4, 128) for r in results)


def shards(queries, keys_in, values, cotangent):
    return pack(exchange(queries, keys_in, values, cotangent))


def solution(mesh):
    in_specs = (P(("seq", "head"), None, None),) * 4
    out_specs = (P("seq", "head", None),) * 4
    return jax.shard_map(shards, mesh=mesh, in_specs=in_specs, out_specs=out_specs, check_vma=False)
```
